128 devices in a mesh: tm: 32 (over y, z_hi, x), head: 4 (over z_lo, core).
Axes of the slice: x: 4, y: 4, z: 4 (z_hi: 2, z_lo: 2; z = z_hi * 2 + z_lo), core: 2. Of those that a mesh axis runs over, the one named last changes fastest.
Arguments:
- frames: bfloat16 [64, 512, 5120], P('tm', None, 'head'), may hold values from -8 to 8
- taps: float32 [3, 5120], P(None, 'head'), may hold values from -3 to 3
- w_query: bfloat16 [5120, 2560], P(None, 'head')
- w_key: bfloat16 [5120, 2560], P(None, 'head')
- w_value: bfloat16 [5120, 2560], P(None, 'head'), may hold values from -0.078125 to 0.078125
- q_gain: float32 [2560], P('head'), may hold values from 0.5 to 6
- k_gain: float32 [2560], P('head'), may hold values from 0.5 to 6
Outputs:
- attended: bfloat16 [64, 512, 2560], P('tm', None, 'head')
The draws below stay inside these ranges and needn't reach their ends.
All inputs are finite; a program needn't handle non-finite values.
Results may differ from the reference program's by a relative error of at most 0.0086.
Values may be sent and summed in bfloat16 or wider, within the bound.
A program may use at most 192 MiB of HBM per device.

```python
import jax
import jax.numpy as jnp
from jax import lax

D = 5120
DH = 128
HEADS = 20
TOK = 512
FRAMES = 64


def shared_weight(key):
    base = jax.random.normal(jax.random.fold_in(key, 11), (D, HEADS * DH), jnp.float32)
    return jnp.clip(base, -4.0, 4.0) * D ** (-0.5)


def draw_w_key(key, part):
    return shared_weight(key).astype(jnp.bfloat16)


def draw_w_query(key, part):
    own_part = jnp.clip(jax.random.normal(jax.random.fold_in(key, 12), (D, HEADS * DH), jnp.float32), -4.0, 4.0) * D ** (-0.5)
    return own_part.astype(jnp.bfloat16)


def draw_frames(key, part):
    drawn = jax.random.normal(jax.random.fold_in(key, 24), (FRAMES, TOK, D), jnp.float32)
    return jnp.clip(drawn, -6.0, 6.0).astype(jnp.bfloat16)


def gain_draw(key, salt):
    return jax.random.uniform(jax.random.fold_in(key, salt), (HEADS * DH,), jnp.float32, 0.5, 1.5)


def draw_q_gain(key, part):
    return gain_draw(key, 31)


def draw_k_gain(key, part):
    return gain_draw(key, 32)


def levels(own_key, shape, split, low, high):
    factor_of = 1.0
    for position, parts in split:
        draws = jax.random.uniform(jax.random.fold_in(jax.random.fold_in(own_key, 6), position), (parts,), jnp.float32, low / len(split), high / len(split))
        factor_of = factor_of * jnp.repeat(jnp.exp(draws), shape[position] // parts).reshape((-1,) + (1,) * (len(shape) - 1 - position))
    return factor_of


def scatter_about(rng, extent, scale, reach, pieces=(), dtype=jnp.bfloat16):
    level = levels(rng, extent, pieces, -0.22, 0.18) if pieces else 1.0
    entries = jax.random.normal(rng, extent, jnp.float32) * scale * level
    return jnp.minimum(jnp.maximum(entries, -reach), reach).astype(dtype)


def setup_inputs(seed: int = 0) -> dict:
    splits = jax.random.split(jax.random.key(seed), 8)
    frames = draw_frames(jax.random.fold_in(splits[7], 71), 0)
    taps = scatter_about(splits[1], (3, D), 0.5, 3.0, ((1, 4),), jnp.float32)
    w_query = draw_w_query(jax.random.fold_in(splits[7], 71), 0)
    w_key = draw_w_key(jax.random.fold_in(splits[7], 71), 0)
    w_value = scatter_about(splits[4], (D, HEADS * DH), D ** -0.5, 0.078125, ((1, 4),))
    q_gain = draw_q_gain(jax.random.fold_in(splits[7], 71), 0)
    k_gain = draw_k_gain(jax.random.fold_in(splits[7], 71), 0)
    return dict(frames=frames, taps=taps, w_query=w_query, w_key=w_key, w_value=w_value, q_gain=q_gain, k_gain=k_gain)


def normalize(projected, gain):
    split_heads = projected.reshape(projected.shape[0], HEADS, DH)
    mean_sq = lax.optimization_barrier(jnp.mean(split_heads * split_heads, axis=-1, keepdims=True))
    scaled = split_heads * lax.rsqrt(mean_sq + 1e-06)
    return scaled.reshape(projected.shape[0], HEADS * DH) * gain

def reference(frames, taps, w_query, w_key, w_value, q_gain, k_gain):
    frame_f = frames.astype(jnp.float32)
    zero_frame = jnp.zeros_like(frame_f[:1])
    before = jnp.concatenate([zero_frame, frame_f[:-1]], axis=0)
    after = jnp.concatenate([frame_f[1:], zero_frame], axis=0)
    mixed = (frame_f + taps[0] * before + taps[1] * frame_f + taps[2] * after).astype(jnp.bfloat16)
    tok_rows = mixed.reshape(FRAMES * TOK, D)
    q_raw = jnp.dot(tok_rows, w_query, preferred_element_type=jnp.float32)
    k_raw = jnp.dot(tok_rows, w_key, preferred_element_type=jnp.float32)
    v_raw = jnp.dot(tok_rows, w_value, preferred_element_type=jnp.float32)
    query = normalize(q_raw, q_gain).astype(jnp.bfloat16).reshape(FRAMES, TOK, HEADS, DH)
    keys = normalize(k_raw, k_gain).astype(jnp.bfloat16).reshape(FRAMES, TOK, HEADS, DH)
    values = v_raw.astype(jnp.bfloat16).reshape(FRAMES, TOK, HEADS, DH)
    prev_keys = jnp.concatenate([keys[:1], keys[:-1]], axis=0)
    prev_values = jnp.concatenate([values[:1], values[:-1]], axis=0)
    anchor_k = keys[0]
    anchor_v = values[0]
    scale = 1.0 / DH ** 0.5

    def frame_attend(items):
        q_frame, k_prev, v_prev = items
        ctx_keys = jnp.concatenate([anchor_k, k_prev], axis=0)
        ctx_vals = jnp.concatenate([anchor_v, v_prev], axis=0)
        scores = jnp.einsum('qhd,khd->hqk', q_frame.astype(jnp.float32), ctx_keys.astype(jnp.float32)) * scale
        top = lax.optimization_barrier(jnp.max(scores, axis=-1, keepdims=True))
        expo = jnp.exp(scores - top)
        probs = (expo / lax.optimization_barrier(jnp.sum(expo, axis=-1, keepdims=True))).astype(jnp.bfloat16)
        out_frame = jnp.einsum('hqk,khd->qhd', probs.astype(jnp.float32), ctx_vals.astype(jnp.float32))
        return out_frame.astype(jnp.bfloat16).reshape(TOK, HEADS * DH)
    return lax.map(frame_attend, (query, prev_keys, prev_values))
```

```python
import functools
import math

import jax
import jax.numpy as jnp
from jax import lax
from jax.experimental import pallas as pl
from jax.experimental.pallas import tpu as pltpu
from jax.sharding import PartitionSpec as P

DH = 128
MESH = pl.DeviceIdType.MESH
F32 = jnp.float32
BF16 = jnp.bfloat16

NX = 4
ROW = 2 * NX
PIECES = 16
STEP = 128
GROUP = 256


def kernel(frames, taps, gain_kv, gain_q, wq, wk, wv, out, XF, M, W, KVB, Q,
           w_sem, f_sem, hs, hr, zs, zr, cs, cr, fs, fr, ks, kr, ls, bs, pr):
    n_tm = lax.axis_size("tm")
    t = lax.axis_index("tm")
    h = lax.axis_index("head")
    tok = frames.shape[1]
    ch = frames.shape[2]
    cols = wq.shape[1]
    heads = cols // DH
    chunks = tok // STEP
    halves = tok // GROUP
    piece_rows = tok // PIECES

    is_first = t == 0
    is_last = t == n_tm - 1
    x_pos = lax.rem(t, NX)
    z_hi = lax.rem(t // NX, 2)
    pos = (t // ROW) * NX + x_pos
    up = lax.rem(t + 1, n_tm)
    down = lax.rem(t + n_tm - 1, n_tm)
    z_slot = lax.rem(h + 2, 4)
    c_slot = h + 1 - 2 * lax.rem(h, 2)
    f_slot = lax.rem(c_slot + 2, 4)
    other = t + NX - 2 * NX * z_hi

    def member(j, plane):
        return (j // NX) * ROW + plane * NX + lax.rem(j, NX)

    def frame_load(c):
        rows = pl.ds(pl.multiple_of(c * STEP, STEP), STEP)
        return pltpu.make_async_copy(frames.at[:, rows, :], XF.at[pl.ds(1, 2), rows, :], f_sem.at[c])

    for c in range(chunks):
        frame_load(c).start()
    w_loads = [
        pltpu.make_async_copy(w, W.at[:, pl.ds(i * cols, cols)], w_sem.at[i])
        for i, w in enumerate((wk, wv, wq))
    ]
    for load in w_loads:
        load.start()

    barrier = pltpu.get_barrier_semaphore()

    def hello(tm, head):
        pl.semaphore_signal(barrier, inc=1, device_id=(tm, head), device_id_type=MESH)

    hello(t, z_slot)
    hello(t, c_slot)
    hello(other, h)

    @pl.loop(0, PIECES)
    def _(j):
        @pl.when(j != pos)
        def _():
            hello(member(j, z_hi), h)

    far_up = jnp.logical_and(x_pos == NX - 1, t < n_tm - 1)
    far_down = jnp.logical_and(x_pos == 0, t > 0)

    @pl.when(far_up)
    def _():
        hello(up, h)

    @pl.when(far_down)
    def _():
        hello(down, h)

    pl.semaphore_wait(barrier, PIECES + 2 + far_up.astype(jnp.int32) + far_down.astype(jnp.int32))

    def halo(side, c):
        rows = pl.ds(pl.multiple_of(c * STEP, STEP), STEP)
        return pltpu.make_async_remote_copy(
            src_ref=frames.at[1 - side, rows, :],
            dst_ref=XF.at[3 * side, rows, :],
            send_sem=hs.at[side, c],
            recv_sem=hr.at[side, c],
            device_id=(down if side else up, h),
            device_id_type=MESH,
        )

    @pl.when(t > 0)
    def _():
        for c in range(chunks):
            halo(1, c).start()

    @pl.when(t < n_tm - 1)
    def _():
        for c in range(chunks):
            halo(0, c).start()

    @pl.when(is_first)
    def _():
        XF[0] = jnp.zeros((tok, ch), BF16)

    @pl.when(is_last)
    def _():
        XF[3] = jnp.zeros((tok, ch), BF16)

    def frame_of(phase):
        return jnp.where(is_first, phase, 1 - phase)

    def block(s):
        return pl.ds(pl.multiple_of(frame_of(s // chunks) * tok + lax.rem(s, chunks) * STEP, STEP), STEP)

    def remote(src, dst, send, recv, tm, head):
        return pltpu.make_async_remote_copy(
            src_ref=src, dst_ref=dst, send_sem=send, recv_sem=recv, device_id=(tm, head), device_id_type=MESH
        )

    def z_copy(s):
        ref = M.at[h, block(s), :]
        return remote(ref, ref, zs.at[s], zr.at[s], t, z_slot)

    def c_copy(s):
        ref = M.at[h, block(s), :]
        return remote(ref, ref, cs.at[s], cr.at[s], t, c_slot)

    def f_copy(s):
        ref = M.at[z_slot, block(s), :]
        return remote(ref, ref, fs.at[s], fr.at[s], t, c_slot)

    def convolve(s):
        frame = frame_of(s // chunks)
        c = lax.rem(s, chunks)

        @pl.when(s < chunks)
        def _():
            frame_load(c).wait()

        @pl.when(jnp.logical_and(frame == 1, t < n_tm - 1))
        def _():
            halo(1, c).wait_recv()

        @pl.when(jnp.logical_and(frame == 0, t > 0))
        def _():
            halo(0, c).wait_recv()

        rows_each = 32

        @pl.loop(0, STEP // rows_each)
        def _(i):
            start = pl.multiple_of(c * STEP + i * rows_each, rows_each)
            rows = pl.ds(start, rows_each)
            centre = XF[frame + 1, rows, :].astype(F32)
            before = XF[frame, rows, :].astype(F32)
            after = XF[frame + 2, rows, :].astype(F32)
            mixed = centre + taps[0:1, :] * before + taps[1:2, :] * centre + taps[2:3, :] * after
            into = pl.ds(pl.multiple_of(frame * tok + start, rows_each), rows_each)
            M[h, into, :] = mixed.astype(BF16)

        z_copy(s).start()
        c_copy(s).start()

    def scaled(raw, gain):
        mean_sq = jnp.mean(raw * raw, axis=-1, keepdims=True)
        return raw * lax.rsqrt(mean_sq + 1e-06) * gain

    def project(rows, col0, width):
        total = None
        for slot in range(4):
            term = jnp.dot(
                M[slot, rows, :], W[pl.ds(slot * ch, ch), pl.ds(col0, width)], preferred_element_type=F32
            )
            total = term if total is None else total + term
        return total

    @pl.loop(0, 2)
    def _(s):
        convolve(s)

    anchor_slot = jnp.where(is_first, 1, 3)

    def kv_copy(half):
        rows = pl.ds(pl.multiple_of(half * GROUP, GROUP), GROUP)
        return remote(KVB.at[2, rows, :], KVB.at[0, rows, :], ks.at[half], kr.at[half], up, h)

    def piece(j):
        return pl.ds(pl.multiple_of(j * piece_rows, piece_rows), piece_rows)

    def scatter_copy(j):
        return remote(KVB.at[1, piece(j), :], KVB.at[3, piece(j), :], ls.at[j], pr.at[j], member(j, 0), h)

    def fan_copy(j, tm):
        return remote(KVB.at[anchor_slot, piece(pos), :], KVB.at[3, piece(pos), :], bs.at[j], pr.at[pos], tm, h)

    def await_piece(j):
        return remote(KVB.at[3, piece(j), :], KVB.at[3, piece(j), :], ls.at[j], pr.at[j], other, h)

    def fan_out(act):
        @pl.loop(0, PIECES)
        def _(j):
            to_plane = jnp.logical_and(j != pos, jnp.logical_or(j != 0, z_hi == 1))

            @pl.when(to_plane)
            def _():
                act(fan_copy(j, member(j, z_hi)))

        @pl.when(z_hi == 0)
        def _():
            act(fan_copy(pos, other))

    @pl.loop(0, 2 * halves)
    def _(g):
        @pl.when(g < 2 * halves - 1)
        def _():
            @pl.loop(0, 2)
            def _(i):
                convolve(2 * g + 2 + i)

        @pl.loop(0, 2)
        def _(i):
            s = 2 * g + i
            z_ref = M.at[z_slot, block(s), :]
            remote(z_ref, z_ref, zs.at[s], zr.at[s], t, z_slot).wait_recv()
            f_copy(s).start()

        @pl.loop(0, 2)
        def _(i):
            s = 2 * g + i
            c_ref = M.at[c_slot, block(s), :]
            remote(c_ref, c_ref, cs.at[s], cr.at[s], t, c_slot).wait_recv()
            f_ref = M.at[f_slot, block(s), :]
            remote(f_ref, f_ref, fs.at[s], fr.at[s], t, c_slot).wait_recv()

        @pl.when(g == 0)
        def _():
            for load in w_loads:
                load.wait()

        frame = frame_of(g // halves)
        half = lax.rem(g, halves)
        m_rows = pl.ds(pl.multiple_of(frame * tok + half * GROUP, GROUP), GROUP)
        k_rows = pl.ds(pl.multiple_of(half * GROUP, GROUP), GROUP)

        @pl.loop(0, heads)
        def _(n):
            col0 = pl.multiple_of(n * 2 * DH, 2 * DH)
            raw = project(m_rows, col0, 2 * DH)
            for i in range(2):
                part = raw[:, i * DH : (i + 1) * DH]
                at = pl.ds(pl.multiple_of(col0 + i * DH, DH), DH)
                normed = scaled(part, gain_kv[:, at])
                keep = jnp.where(2 * n + i < heads, normed, part)
                KVB[frame + 1, k_rows, at] = keep.astype(BF16)

        @pl.loop(0, heads // 2)
        def _(n):
            col0 = pl.multiple_of(n * 2 * DH, 2 * DH)
            raw = project(m_rows, 2 * cols + col0, 2 * DH)
            for i in range(2):
                at = pl.ds(pl.multiple_of(col0 + i * DH, DH), DH)
                Q[m_rows, at] = scaled(raw[:, i * DH : (i + 1) * DH], gain_q[:, at]).astype(BF16)

        if heads % 2:
            at = pl.ds((heads - 1) * DH, DH)
            raw = project(m_rows, 2 * cols + (heads - 1) * DH, DH)
            Q[m_rows, at] = scaled(raw, gain_q[:, at]).astype(BF16)

        @pl.when(jnp.logical_and(frame == 1, t < n_tm - 1))
        def _():
            kv_copy(half).start()

        @pl.when(jnp.logical_and(frame == 0, is_first))
        def _():
            each = PIECES // halves

            @pl.loop(0, each)
            def _(i):
                j = half * each + i

                @pl.when(j > 0)
                def _():
                    scatter_copy(j).start()

        @pl.when(jnp.logical_and(g == 1, z_hi == 0))
        def _():
            @pl.when(t > 0)
            def _():
                await_piece(pos).wait_recv()

            fan_out(lambda copy: copy.start())

        @pl.when(jnp.logical_and(g == 2, z_hi == 1))
        def _():
            await_piece(pos).wait_recv()
            fan_out(lambda copy: copy.start())

    @pl.when(t > 0)
    def _():
        @pl.loop(0, PIECES)
        def _(j):
            @pl.when(j != pos)
            def _():
                await_piece(j).wait_recv()

    factor = math.log2(math.e) / DH**0.5

    def attend(frame, prev_slot):
        @pl.loop(0, heads * halves)
        def _(i):
            head = i // halves
            block_q = lax.rem(i, halves)
            k_at = pl.ds(pl.multiple_of(head * DH, DH), DH)
            v_at = pl.ds(pl.multiple_of(cols + head * DH, DH), DH)
            q = Q[pl.ds(pl.multiple_of(frame * tok + block_q * GROUP, GROUP), GROUP), k_at]
            dims = (((1,), (1,)), ((), ()))
            s0 = lax.dot_general(q, KVB[anchor_slot, :, k_at], dims, preferred_element_type=F32)
            s1 = lax.dot_general(q, KVB[prev_slot, :, k_at], dims, preferred_element_type=F32)
            top = jnp.maximum(jnp.max(s0, axis=-1, keepdims=True), jnp.max(s1, axis=-1, keepdims=True))
            e0 = jnp.exp2((s0 - top) * factor)
            e1 = jnp.exp2((s1 - top) * factor)
            norm = jnp.sum(e0, axis=-1, keepdims=True) + jnp.sum(e1, axis=-1, keepdims=True)
            acc = jnp.dot(e0.astype(BF16), KVB[anchor_slot, :, v_at], preferred_element_type=F32)
            acc += jnp.dot(e1.astype(BF16), KVB[prev_slot, :, v_at], preferred_element_type=F32)
            out[frame, pl.ds(pl.multiple_of(block_q * GROUP, GROUP), GROUP), k_at] = (acc / norm).astype(BF16)

    attend(1, 1)

    @pl.when(t > 0)
    def _():
        for half in range(halves):
            kv_copy(half).wait_recv()

    attend(0, jnp.where(is_first, 1, 0))

    @pl.loop(0, 2 * chunks)
    def _(s):
        z_copy(s).wait_send()
        c_copy(s).wait_send()
        f_copy(s).wait_send()

    @pl.when(t > 0)
    def _():
        for c in range(chunks):
            halo(1, c).wait_send()

    @pl.when(t < n_tm - 1)
    def _():
        for c in range(chunks):
            halo(0, c).wait_send()
        for half in range(halves):
            kv_copy(half).wait_send()

    @pl.when(is_first)
    def _():
        @pl.loop(1, PIECES)
        def _(j):
            scatter_copy(j).wait_send()

    fan_out(lambda copy: copy.wait_send())


def per_device(frames, taps, w_query, w_key, w_value, q_gain, k_gain):
    count, tok, ch = frames.shape
    depth, cols = w_query.shape
    chunks = tok // STEP
    halves = tok // GROUP
    gain_kv = jnp.concatenate([k_gain, jnp.ones_like(k_gain)])[None]
    gain_q = q_gain[None]
    dma = pltpu.SemaphoreType.DMA
    vmem = pl.BlockSpec(memory_space=pltpu.VMEM)
    anywhere = pl.BlockSpec(memory_space=pl.ANY)
    return pl.pallas_call(
        kernel,
        out_shape=jax.ShapeDtypeStruct((count, tok, cols), BF16),
        in_specs=[anywhere, vmem, vmem, vmem, anywhere, anywhere, anywhere],
        out_specs=vmem,
        scratch_shapes=[
            pltpu.VMEM((4, tok, ch), BF16),
            pltpu.VMEM((4, count * tok, ch), BF16),
            pltpu.VMEM((depth, 3 * cols), BF16),
            pltpu.VMEM((4, tok, 2 * cols), BF16),
            pltpu.VMEM((count * tok, cols), BF16),
            dma((3,)),
            dma((chunks,)),
            dma((2, chunks)),
            dma((2, chunks)),
            dma((2 * chunks,)),
            dma((2 * chunks,)),
            dma((2 * chunks,)),
            dma((2 * chunks,)),
            dma((2 * chunks,)),
            dma((2 * chunks,)),
            dma((halves,)),
            dma((halves,)),
            dma((PIECES,)),
            dma((PIECES,)),
            dma((PIECES,)),
        ],
        compiler_params=pltpu.CompilerParams(
            collective_id=0, has_side_effects=True, vmem_limit_bytes=62 * 1024 * 1024
        ),
    )(frames, taps, gain_kv, gain_q, w_query, w_key, w_value)


def solution(mesh):
    placed = (
        P("tm", None, "head"),
        P(None, "head"),
        P(None, "head"),
        P(None, "head"),
        P(None, "head"),
        P("head"),
        P("head"),
    )
    return jax.shard_map(
        per_device, mesh=mesh, in_specs=placed, out_specs=P("tm", None, "head"), check_vma=False
    )
```

```python
import functools
import math

import jax
import jax.numpy as jnp
from jax import lax
from jax.experimental import pallas as pl
from jax.experimental.pallas import tpu as pltpu
from jax.sharding import PartitionSpec as P

DH = 128
MESH = pl.DeviceIdType.MESH
F32 = jnp.float32
BF16 = jnp.bfloat16

NX = 4
ROW = 2 * NX
PIECES = 16
STEP = 128
GROUP = 256


def kernel(frames, taps, gain_kv, gain_q, wq, wk, wv, out, XF, M, W, KVB, Q, KVR,
           w_sem, f_sem, hs, hr, zs, zr, cs, cr, fs, fr, ks, kr, rs, rr, ls, bs, pr):
    n_tm = lax.axis_size("tm")
    t = lax.axis_index("tm")
    h = lax.axis_index("head")
    tok = frames.shape[1]
    ch = frames.shape[2]
    cols = wq.shape[1]
    heads = cols // DH
    chunks = tok // STEP
    halves = tok // GROUP
    piece_rows = tok // PIECES

    is_first = t == 0
    is_last = t == n_tm - 1
    x_pos = lax.rem(t, NX)
    z_hi = lax.rem(t // NX, 2)
    pos = (t // ROW) * NX + x_pos
    up = lax.rem(t + 1, n_tm)
    down = lax.rem(t + n_tm - 1, n_tm)
    z_slot = lax.rem(h + 2, 4)
    c_slot = h + 1 - 2 * lax.rem(h, 2)
    f_slot = lax.rem(c_slot + 2, 4)
    row = t // NX
    n_rows = n_tm // NX

    def member(j, plane):
        return (j // NX) * ROW + plane * NX + lax.rem(j, NX)

    def frame_load(c):
        rows = pl.ds(pl.multiple_of(c * STEP, STEP), STEP)
        return pltpu.make_async_copy(frames.at[:, rows, :], XF.at[pl.ds(1, 2), rows, :], f_sem.at[c])

    for c in range(chunks):
        frame_load(c).start()
    w_loads = [
        pltpu.make_async_copy(w, W.at[:, pl.ds(i * cols, cols)], w_sem.at[i])
        for i, w in enumerate((wk, wv, wq))
    ]
    for load in w_loads:
        load.start()

    barrier = pltpu.get_barrier_semaphore()

    def hello(tm, head):
        pl.semaphore_signal(barrier, inc=1, device_id=(tm, head), device_id_type=MESH)

    hello(t, z_slot)
    hello(t, c_slot)

    @pl.loop(0, PIECES)
    def _(j):
        @pl.when(j != pos)
        def _():
            hello(member(j, z_hi), h)

        @pl.when(is_first)
        def _():
            hello(member(j, 1), h)

    has_next = jnp.logical_and(x_pos == NX - 1, t < n_tm - 1)
    has_prev = jnp.logical_and(x_pos == 0, t > 0)
    is_relay = jnp.logical_and(jnp.logical_and(x_pos > 0, x_pos < NX - 1), row > 0)

    @pl.when(has_next)
    def _():
        for i in range(1, NX):
            hello(t + i, h)

    @pl.when(has_prev)
    def _():
        hello(down, h)

    @pl.when(is_relay)
    def _():
        hello(row * NX - 1, h)

    @pl.when(z_hi == 1)
    def _():
        hello(0, h)

    expected = PIECES + 1 + z_hi
    for cond, count in ((has_next, NX - 1), (has_prev, 1), (is_relay, 1), (is_first, PIECES)):
        expected = expected + jnp.where(cond, count, 0)
    pl.semaphore_wait(barrier, expected)

    def halo(side, c):
        rows = pl.ds(pl.multiple_of(c * STEP, STEP), STEP)
        return pltpu.make_async_remote_copy(
            src_ref=frames.at[1 - side, rows, :],
            dst_ref=XF.at[3 * side, rows, :],
            send_sem=hs.at[side, c],
            recv_sem=hr.at[side, c],
            device_id=(down if side else up, h),
            device_id_type=MESH,
        )

    @pl.when(t > 0)
    def _():
        for c in range(chunks):
            halo(1, c).start()

    @pl.when(t < n_tm - 1)
    def _():
        for c in range(chunks):
            halo(0, c).start()

    @pl.when(is_first)
    def _():
        XF[0] = jnp.zeros((tok, ch), BF16)

    @pl.when(is_last)
    def _():
        XF[3] = jnp.zeros((tok, ch), BF16)

    def frame_of(phase):
        return jnp.where(is_first, phase, 1 - phase)

    def block(s):
        return pl.ds(pl.multiple_of(frame_of(s // chunks) * tok + lax.rem(s, chunks) * STEP, STEP), STEP)

    def remote(src, dst, send, recv, tm, head):
        return pltpu.make_async_remote_copy(
            src_ref=src, dst_ref=dst, send_sem=send, recv_sem=recv, device_id=(tm, head), device_id_type=MESH
        )

    def z_copy(s):
        ref = M.at[h, block(s), :]
        return remote(ref, ref, zs.at[s], zr.at[s], t, z_slot)

    def c_copy(s):
        ref = M.at[h, block(s), :]
        return remote(ref, ref, cs.at[s], cr.at[s], t, c_slot)

    def f_copy(s):
        ref = M.at[z_slot, block(s), :]
        return remote(ref, ref, fs.at[s], fr.at[s], t, c_slot)

    def convolve(s):
        frame = frame_of(s // chunks)
        c = lax.rem(s, chunks)

        @pl.when(s < chunks)
        def _():
            frame_load(c).wait()

        @pl.when(jnp.logical_and(frame == 1, t < n_tm - 1))
        def _():
            halo(1, c).wait_recv()

        @pl.when(jnp.logical_and(frame == 0, t > 0))
        def _():
            halo(0, c).wait_recv()

        rows_each = 32

        @pl.loop(0, STEP // rows_each)
        def _(i):
            start = pl.multiple_of(c * STEP + i * rows_each, rows_each)
            rows = pl.ds(start, rows_each)
            centre = XF[frame + 1, rows, :].astype(F32)
            before = XF[frame, rows, :].astype(F32)
            after = XF[frame + 2, rows, :].astype(F32)
            mixed = centre + taps[0:1, :] * before + taps[1:2, :] * centre + taps[2:3, :] * after
            into = pl.ds(pl.multiple_of(frame * tok + start, rows_each), rows_each)
            M[h, into, :] = mixed.astype(BF16)

        z_copy(s).start()
        c_copy(s).start()

    def scaled(raw, gain):
        mean_sq = jnp.mean(raw * raw, axis=-1, keepdims=True)
        return raw * lax.rsqrt(mean_sq + 1e-06) * gain

    def project(rows, col0, width):
        total = None
        for slot in range(4):
            term = jnp.dot(
                M[slot, rows, :], W[pl.ds(slot * ch, ch), pl.ds(col0, width)], preferred_element_type=F32
            )
            total = term if total is None else total + term
        return total

    @pl.loop(0, 2)
    def _(s):
        convolve(s)

    anchor_slot = jnp.where(is_first, 1, 3)

    def half_rows(half):
        return pl.ds(pl.multiple_of(half * GROUP, GROUP), GROUP)

    def kv_copy(half):
        rows = half_rows(half)
        return remote(KVB.at[2, rows, :], KVB.at[0, rows, :], ks.at[half], kr.at[half], up, h)

    def relay_in(half):
        return remote(KVB.at[2, half_rows(half), :], KVR, ks.at[half], rr.at[0], lax.rem(t + 2 + half, n_tm), h)

    def relay_out(half):
        return remote(KVR, KVB.at[0, half_rows(half), :], rs.at[0], kr.at[half], row * NX, h)

    def send_kv(half, act):
        @pl.when(has_next)
        def _():
            act(relay_in(half))

        @pl.when(x_pos < NX - 1)
        def _():
            act(kv_copy(half))

    def piece(j):
        return pl.ds(pl.multiple_of(j * piece_rows, piece_rows), piece_rows)

    def scatter_copy(j, plane):
        return remote(KVB.at[1, piece(j), :], KVB.at[3, piece(j), :], ls.at[plane, j], pr.at[j], member(j, plane), h)

    def fan_copy(j):
        return remote(
            KVB.at[anchor_slot, piece(pos), :], KVB.at[3, piece(pos), :], bs.at[j], pr.at[pos], member(j, z_hi), h
        )

    def await_piece(j):
        return remote(KVB.at[3, piece(j), :], KVB.at[3, piece(j), :], ls.at[0, j], pr.at[j], member(j, 1 - z_hi), h)

    def fan_out(act):
        @pl.loop(0, PIECES)
        def _(j):
            @pl.when(jnp.logical_and(j != pos, jnp.logical_or(j != 0, z_hi == 1)))
            def _():
                act(fan_copy(j))

    each = PIECES // halves

    def scatter(half, act):
        @pl.loop(0, each)
        def _(i):
            j = half * each + i

            @pl.when(j > 0)
            def _():
                act(scatter_copy(j, 0))

            act(scatter_copy(j, 1))

    def qkv(frame, first, count):
        m_rows = pl.ds(pl.multiple_of(frame * tok + first, count), count)
        k_rows = pl.ds(pl.multiple_of(first, count), count)

        @pl.loop(0, heads)
        def _(n):
            col0 = pl.multiple_of(n * 2 * DH, 2 * DH)
            raw = project(m_rows, col0, 2 * DH)
            for i in range(2):
                part = raw[:, i * DH : (i + 1) * DH]
                at = pl.ds(pl.multiple_of(col0 + i * DH, DH), DH)
                normed = scaled(part, gain_kv[:, at])
                keep = jnp.where(2 * n + i < heads, normed, part)
                KVB[frame + 1, k_rows, at] = keep.astype(BF16)

        @pl.loop(0, heads // 2)
        def _(n):
            col0 = pl.multiple_of(n * 2 * DH, 2 * DH)
            raw = project(m_rows, 2 * cols + col0, 2 * DH)
            for i in range(2):
                at = pl.ds(pl.multiple_of(col0 + i * DH, DH), DH)
                Q[m_rows, at] = scaled(raw[:, i * DH : (i + 1) * DH], gain_q[:, at]).astype(BF16)

        if heads % 2:
            at = pl.ds((heads - 1) * DH, DH)
            raw = project(m_rows, 2 * cols + (heads - 1) * DH, DH)
            Q[m_rows, at] = scaled(raw, gain_q[:, at]).astype(BF16)

    def forward(s):
        z_ref = M.at[z_slot, block(s), :]
        remote(z_ref, z_ref, zs.at[s], zr.at[s], t, z_slot).wait_recv()
        f_copy(s).start()

    def gathered(s):
        c_ref = M.at[c_slot, block(s), :]
        remote(c_ref, c_ref, cs.at[s], cr.at[s], t, c_slot).wait_recv()
        f_ref = M.at[f_slot, block(s), :]
        remote(f_ref, f_ref, fs.at[s], fr.at[s], t, c_slot).wait_recv()

    groups = 2 * halves

    @pl.loop(0, groups - 1)
    def _(g):
        @pl.loop(0, 2)
        def _(i):
            convolve(2 * g + 2 + i)

        @pl.loop(0, 2)
        def _(i):
            forward(2 * g + i)

        @pl.loop(0, 2)
        def _(i):
            gathered(2 * g + i)

        @pl.when(g == 0)
        def _():
            for load in w_loads:
                load.wait()

        frame = frame_of(g // halves)
        half = lax.rem(g, halves)
        qkv(frame, half * GROUP, GROUP)

        @pl.when(jnp.logical_and(frame == 1, t < n_tm - 1))
        def _():
            send_kv(half, lambda copy: copy.start())

        @pl.when(jnp.logical_and(frame == 0, is_first))
        def _():
            scatter(half, lambda copy: copy.start())

        @pl.when(jnp.logical_and(is_relay, g == x_pos))
        def _():
            relay_in(x_pos - 1).wait_recv()
            relay_out(x_pos - 1).start()

        @pl.when(g == 1 + pos // each)
        def _():
            @pl.when(t > 0)
            def _():
                await_piece(pos).wait_recv()

            fan_out(lambda copy: copy.start())

    @pl.loop(2 * groups - 2, 2 * groups)
    def _(s):
        forward(s)
        gathered(s)
        qkv(frame_of(1), lax.rem(s, chunks) * STEP, STEP)

    @pl.when(is_first)
    def _():
        send_kv(halves - 1, lambda copy: copy.start())

    @pl.when(t > 0)
    def _():
        @pl.loop(0, PIECES)
        def _(j):
            @pl.when(j != pos)
            def _():
                await_piece(j).wait_recv()

    factor = math.log2(math.e) / DH**0.5

    def attend(frame, prev_slot):
        @pl.loop(0, heads * halves)
        def _(i):
            head = i // halves
            block_q = lax.rem(i, halves)
            k_at = pl.ds(pl.multiple_of(head * DH, DH), DH)
            v_at = pl.ds(pl.multiple_of(cols + head * DH, DH), DH)
            q = Q[pl.ds(pl.multiple_of(frame * tok + block_q * GROUP, GROUP), GROUP), k_at]
            dims = (((1,), (1,)), ((), ()))
            s0 = lax.dot_general(q, KVB[anchor_slot, :, k_at], dims, preferred_element_type=F32)
            s1 = lax.dot_general(q, KVB[prev_slot, :, k_at], dims, preferred_element_type=F32)
            top = jnp.maximum(jnp.max(s0, axis=-1, keepdims=True), jnp.max(s1, axis=-1, keepdims=True))
            e0 = jnp.exp2((s0 - top) * factor)
            e1 = jnp.exp2((s1 - top) * factor)
            norm = jnp.sum(e0, axis=-1, keepdims=True) + jnp.sum(e1, axis=-1, keepdims=True)
            acc = jnp.dot(e0.astype(BF16), KVB[anchor_slot, :, v_at], preferred_element_type=F32)
            acc += jnp.dot(e1.astype(BF16), KVB[prev_slot, :, v_at], preferred_element_type=F32)
            out[frame, pl.ds(pl.multiple_of(block_q * GROUP, GROUP), GROUP), k_at] = (acc / norm).astype(BF16)

    attend(1, 1)

    @pl.when(t > 0)
    def _():
        for half in range(halves):
            kv_copy(half).wait_recv()

    attend(0, jnp.where(is_first, 1, 0))

    @pl.loop(0, 2 * chunks)
    def _(s):
        z_copy(s).wait_send()
        c_copy(s).wait_send()
        f_copy(s).wait_send()

    @pl.when(t > 0)
    def _():
        for c in range(chunks):
            halo(1, c).wait_send()

    @pl.when(t < n_tm - 1)
    def _():
        for c in range(chunks):
            halo(0, c).wait_send()
        for half in range(halves):
            send_kv(half, lambda copy: copy.wait_send())

    @pl.when(is_relay)
    def _():
        relay_out(x_pos - 1).wait_send()

    @pl.when(is_first)
    def _():
        for half in range(halves):
            scatter(half, lambda copy: copy.wait_send())

    fan_out(lambda copy: copy.wait_send())


def per_device(frames, taps, w_query, w_key, w_value, q_gain, k_gain):
    count, tok, ch = frames.shape
    depth, cols = w_query.shape
    chunks = tok // STEP
    halves = tok // GROUP
    gain_kv = jnp.concatenate([k_gain, jnp.ones_like(k_gain)])[None]
    gain_q = q_gain[None]
    dma = pltpu.SemaphoreType.DMA
    vmem = pl.BlockSpec(memory_space=pltpu.VMEM)
    anywhere = pl.BlockSpec(memory_space=pl.ANY)
    return pl.pallas_call(
        kernel,
        out_shape=jax.ShapeDtypeStruct((count, tok, cols), BF16),
        in_specs=[anywhere, vmem, vmem, vmem, anywhere, anywhere, anywhere],
        out_specs=vmem,
        scratch_shapes=[
            pltpu.VMEM((4, tok, ch), BF16),
            pltpu.VMEM((4, count * tok, ch), BF16),
            pltpu.VMEM((depth, 3 * cols), BF16),
            pltpu.VMEM((4, tok, 2 * cols), BF16),
            pltpu.VMEM((count * tok, cols), BF16),
            pltpu.VMEM((GROUP, 2 * cols), BF16),
            dma((3,)),
            dma((chunks,)),
            dma((2, chunks)),
            dma((2, chunks)),
            dma((2 * chunks,)),
            dma((2 * chunks,)),
            dma((2 * chunks,)),
            dma((2 * chunks,)),
            dma((2 * chunks,)),
            dma((2 * chunks,)),
            dma((halves,)),
            dma((halves,)),
            dma((1,)),
            dma((1,)),
            dma((2, PIECES)),
            dma((PIECES,)),
            dma((PIECES,)),
        ],
        compiler_params=pltpu.CompilerParams(
            collective_id=0, has_side_effects=True, vmem_limit_bytes=62 * 1024 * 1024
        ),
    )(frames, taps, gain_kv, gain_q, w_query, w_key, w_value)


def solution(mesh):
    placed = (
        P("tm", None, "head"),
        P(None, "head"),
        P(None, "head"),
        P(None, "head"),
        P(None, "head"),
        P("head"),
        P("head"),
    )
    return jax.shard_map(
        per_device, mesh=mesh, in_specs=placed, out_specs=P("tm", None, "head"), check_vma=False
    )
```

```python
import functools
import math

import jax
import jax.numpy as jnp
from jax import lax
from jax.experimental import pallas as pl
from jax.experimental.pallas import tpu as pltpu
from jax.sharding import PartitionSpec as P

DH = 128
MESH = pl.DeviceIdType.MESH
F32 = jnp.float32
BF16 = jnp.bfloat16

NX = 4
ROW = 2 * NX
PIECES = 16
STEP = 128
GROUP = 256


def kernel(frames, taps, gain_q, gain_k, wq, wk, wv, out, XF, M, W, KVB, Q, KVR, HR,
           w_sem, f_sem, hs, hr, zs, zr, cs, cr, fs, fr, ks, kr, rs, rr, us, ur, ls, bs, pr):
    n_tm = lax.axis_size("tm")
    t = lax.axis_index("tm")
    h = lax.axis_index("head")
    tok = frames.shape[1]
    ch = frames.shape[2]
    cols = wq.shape[1]
    heads = cols // DH
    chunks = tok // STEP
    halves = tok // GROUP
    piece_rows = tok // PIECES

    is_first = t == 0
    is_last = t == n_tm - 1
    x_pos = lax.rem(t, NX)
    z_hi = lax.rem(t // NX, 2)
    pos = (t // ROW) * NX + x_pos
    up = lax.rem(t + 1, n_tm)
    down = lax.rem(t + n_tm - 1, n_tm)
    z_slot = lax.rem(h + 2, 4)
    c_slot = h + 1 - 2 * lax.rem(h, 2)
    f_slot = lax.rem(c_slot + 2, 4)
    row = t // NX
    n_rows = n_tm // NX

    def member(j, plane):
        return (j // NX) * ROW + plane * NX + lax.rem(j, NX)

    def frame_load(c):
        rows = pl.ds(pl.multiple_of(c * STEP, STEP), STEP)
        return pltpu.make_async_copy(frames.at[:, rows, :], XF.at[pl.ds(1, 2), rows, :], f_sem.at[c])

    for c in range(chunks):
        frame_load(c).start()
    w_loads = [
        pltpu.make_async_copy(w, W.at[:, pl.ds(i * cols, cols)], w_sem.at[i])
        for i, w in enumerate((wk, wv, wq))
    ]
    for load in w_loads:
        load.start()

    barrier = pltpu.get_barrier_semaphore()

    def hello(tm, head):
        pl.semaphore_signal(barrier, inc=1, device_id=(tm, head), device_id_type=MESH)

    hello(t, z_slot)
    hello(t, c_slot)

    @pl.loop(0, PIECES)
    def _(j):
        @pl.when(j != pos)
        def _():
            hello(member(j, z_hi), h)

        @pl.when(is_first)
        def _():
            hello(member(j, 1), h)

    has_next = jnp.logical_and(x_pos == NX - 1, t < n_tm - 1)
    has_prev = jnp.logical_and(x_pos == 0, t > 0)
    inner = jnp.logical_and(x_pos > 0, x_pos < NX - 1)
    kv_relay = jnp.logical_and(inner, row > 0)
    down_relay = jnp.logical_and(inner, row < n_rows - 1)
    up_relay = jnp.logical_and(x_pos == NX - 1, row > 0)

    @pl.when(has_next)
    def _():
        for i in range(1, NX + 1):
            hello(t + i, h)

    @pl.when(has_prev)
    def _():
        for i in range(1, NX):
            hello(t - i, h)

    @pl.when(jnp.logical_or(kv_relay, up_relay))
    def _():
        hello(row * NX - 1, h)

    @pl.when(down_relay)
    def _():
        hello(row * NX + NX, h)

    @pl.when(z_hi == 1)
    def _():
        hello(0, h)

    expected = PIECES + 1 + z_hi
    for cond, count in (
        (has_next, NX),
        (has_prev, NX - 1),
        (kv_relay, 1),
        (up_relay, 1),
        (down_relay, 1),
        (is_first, PIECES),
    ):
        expected = expected + jnp.where(cond, count, 0)
    pl.semaphore_wait(barrier, expected)

    def remote(src, dst, send, recv, tm, head):
        return pltpu.make_async_remote_copy(
            src_ref=src, dst_ref=dst, send_sem=send, recv_sem=recv, device_id=(tm, head), device_id_type=MESH
        )

    def step_rows(c):
        return pl.ds(pl.multiple_of(c * STEP, STEP), STEP)

    def halo(side, c):
        rows = step_rows(c)
        to = down if side else up
        return remote(frames.at[1 - side, rows, :], XF.at[3 * side, rows, :], hs.at[side, c], hr.at[side, c], to, h)

    def halo_in(side, c):
        to = lax.rem(t + NX, n_tm) if side == 0 else lax.rem(t - c + n_tm, n_tm)
        return remote(frames.at[1 - side, step_rows(c), :], HR, hs.at[side, c], ur.at[0], to, h)

    def halo_sends(act):
        for c in range(chunks):
            for side, some, far in ((1, t > 0, x_pos == 0), (0, t < n_tm - 1, x_pos == NX - 1)):
                relayed = c >= chunks - (2 if side else 1)

                if relayed:
                    @pl.when(jnp.logical_and(some, far))
                    def _():
                        act(halo_in(side, c))

                    @pl.when(jnp.logical_and(some, jnp.logical_not(far)))
                    def _():
                        act(halo(side, c))
                else:
                    @pl.when(some)
                    def _():
                        act(halo(side, c))

    halo_sends(lambda copy: copy.start())

    def down_out():
        c = chunks - x_pos
        return remote(HR, XF.at[3, step_rows(c), :], us.at[0], hr.at[1, c], row * NX + NX - 1, h)

    def up_out():
        c = chunks - 1
        return remote(HR, XF.at[0, step_rows(c), :], us.at[0], hr.at[0, c], row * NX, h)

    def halo_arrived():
        halo_in(0, chunks - 1).wait_recv()

    @pl.when(is_first)
    def _():
        XF[0] = jnp.zeros((tok, ch), BF16)

    @pl.when(is_last)
    def _():
        XF[3] = jnp.zeros((tok, ch), BF16)

    def frame_of(phase):
        return jnp.where(is_first, phase, 1 - phase)

    def block(s):
        return pl.ds(pl.multiple_of(frame_of(s // chunks) * tok + lax.rem(s, chunks) * STEP, STEP), STEP)

    def z_copy(s):
        ref = M.at[h, block(s), :]
        return remote(ref, ref, zs.at[s], zr.at[s], t, z_slot)

    def c_copy(s):
        ref = M.at[h, block(s), :]
        return remote(ref, ref, cs.at[s], cr.at[s], t, c_slot)

    def f_copy(s):
        ref = M.at[z_slot, block(s), :]
        return remote(ref, ref, fs.at[s], fr.at[s], t, c_slot)

    def convolve(s):
        frame = frame_of(s // chunks)
        c = lax.rem(s, chunks)

        @pl.when(s < chunks)
        def _():
            frame_load(c).wait()

        @pl.when(jnp.logical_and(frame == 1, t < n_tm - 1))
        def _():
            halo(1, c).wait_recv()

        @pl.when(jnp.logical_and(frame == 0, t > 0))
        def _():
            halo(0, c).wait_recv()

        rows_each = 32

        @pl.loop(0, STEP // rows_each)
        def _(i):
            start = pl.multiple_of(c * STEP + i * rows_each, rows_each)
            rows = pl.ds(start, rows_each)
            centre = XF[frame + 1, rows, :].astype(F32)
            before = XF[frame, rows, :].astype(F32)
            after = XF[frame + 2, rows, :].astype(F32)
            mixed = centre + taps[0:1, :] * before + taps[1:2, :] * centre + taps[2:3, :] * after
            into = pl.ds(pl.multiple_of(frame * tok + start, rows_each), rows_each)
            M[h, into, :] = mixed.astype(BF16)

        z_copy(s).start()
        c_copy(s).start()

    def scaled(raw, gain):
        mean_sq = jnp.mean(raw * raw, axis=-1, keepdims=True)
        return raw * lax.rsqrt(mean_sq + 1e-06) * gain

    def project(rows, col0, width):
        total = None
        for slot in range(4):
            term = jnp.dot(
                M[slot, rows, :], W[pl.ds(slot * ch, ch), pl.ds(col0, width)], preferred_element_type=F32
            )
            total = term if total is None else total + term
        return total

    @pl.loop(0, 2)
    def _(s):
        convolve(s)

    anchor_slot = jnp.where(is_first, 1, 3)

    def kv_copy(c):
        rows = step_rows(c)
        return remote(KVB.at[2, rows, :], KVB.at[0, rows, :], ks.at[c], kr.at[c], up, h)

    def relay_in(c):
        to = lax.rem(t + 2 + lax.rem(c, 2), n_tm)
        return remote(KVB.at[2, step_rows(c), :], KVR.at[c // 2], ks.at[c], rr.at[c // 2], to, h)

    def relay_out(half):
        c = 2 * half + x_pos - 1
        return remote(KVR.at[half], KVB.at[0, step_rows(c), :], rs.at[half], kr.at[c], row * NX, h)

    def send_kv(c, act):
        @pl.when(has_next)
        def _():
            act(relay_in(c))

        @pl.when(x_pos < NX - 1)
        def _():
            act(kv_copy(c))

    def pass_kv(half):
        @pl.when(kv_relay)
        def _():
            relay_in(2 * half).wait_recv()
            relay_out(half).start()

    def piece(j):
        return pl.ds(pl.multiple_of(j * piece_rows, piece_rows), piece_rows)

    def scatter_copy(j, plane):
        return remote(KVB.at[1, piece(j), :], KVB.at[3, piece(j), :], ls.at[plane, j], pr.at[j], member(j, plane), h)

    def fan_copy(j):
        return remote(
            KVB.at[anchor_slot, piece(pos), :], KVB.at[3, piece(pos), :], bs.at[j], pr.at[pos], member(j, z_hi), h
        )

    def await_piece(j):
        return remote(KVB.at[3, piece(j), :], KVB.at[3, piece(j), :], ls.at[0, j], pr.at[j], member(j, 1 - z_hi), h)

    def fan_out(act):
        @pl.loop(0, PIECES)
        def _(j):
            @pl.when(jnp.logical_and(j != pos, jnp.logical_or(j != 0, z_hi == 1)))
            def _():
                act(fan_copy(j))

    each = PIECES // halves

    def scatter(half, act):
        @pl.loop(0, each)
        def _(i):
            j = half * each + i

            @pl.when(j > 0)
            def _():
                act(scatter_copy(j, 0))

            act(scatter_copy(j, 1))

    def qkv(frame, first, count):
        m_rows = pl.ds(pl.multiple_of(frame * tok + first, count), count)
        k_rows = pl.ds(pl.multiple_of(first, count), count)

        @pl.loop(0, heads)
        def _(n):
            col0 = pl.multiple_of(n * 2 * DH, 2 * DH)
            raw = project(m_rows, col0, 2 * DH)
            for i in range(2):
                part = raw[:, i * DH : (i + 1) * DH]
                at = pl.ds(pl.multiple_of(col0 + i * DH, DH), DH)
                is_key = 2 * n + i < heads
                at_k = pl.ds(pl.multiple_of(jnp.where(is_key, col0 + i * DH, 0), DH), DH)
                keep = jnp.where(is_key, scaled(part, gain_k[at_k]), part)
                KVB[frame + 1, k_rows, at] = keep.astype(BF16)

        @pl.loop(0, heads // 2)
        def _(n):
            col0 = pl.multiple_of(n * 2 * DH, 2 * DH)
            raw = project(m_rows, 2 * cols + col0, 2 * DH)
            for i in range(2):
                at = pl.ds(pl.multiple_of(col0 + i * DH, DH), DH)
                Q[m_rows, at] = scaled(raw[:, i * DH : (i + 1) * DH], gain_q[at]).astype(BF16)

        if heads % 2:
            at = pl.ds((heads - 1) * DH, DH)
            raw = project(m_rows, 2 * cols + (heads - 1) * DH, DH)
            Q[m_rows, at] = scaled(raw, gain_q[at]).astype(BF16)

    def forward(s):
        z_ref = M.at[z_slot, block(s), :]
        remote(z_ref, z_ref, zs.at[s], zr.at[s], t, z_slot).wait_recv()
        f_copy(s).start()

    def gathered(s):
        c_ref = M.at[c_slot, block(s), :]
        remote(c_ref, c_ref, cs.at[s], cr.at[s], t, c_slot).wait_recv()
        f_ref = M.at[f_slot, block(s), :]
        remote(f_ref, f_ref, fs.at[s], fr.at[s], t, c_slot).wait_recv()

    groups = 2 * halves

    @pl.when(down_relay)
    def _():
        halo_arrived()
        down_out().start()

    @pl.loop(0, groups - 1)
    def _(g):
        convolve(2 * g + 2)

        @pl.loop(0, 2)
        def _(i):
            forward(2 * g + i)

        @pl.loop(0, 2)
        def _(i):
            gathered(2 * g + i)

        convolve(2 * g + 3)

        @pl.when(g == 0)
        def _():
            for load in w_loads:
                load.wait()

            @pl.when(up_relay)
            def _():
                halo_arrived()
                up_out().start()

        @pl.when(g == 1 + pos // each)
        def _():
            @pl.when(t > 0)
            def _():
                await_piece(pos).wait_recv()

            fan_out(lambda copy: copy.start())

        @pl.when(g == 2)
        def _():
            pass_kv(0)

        frame = frame_of(g // halves)
        half = lax.rem(g, halves)
        qkv(frame, half * GROUP, GROUP)

        @pl.when(jnp.logical_and(frame == 1, t < n_tm - 1))
        def _():
            send_kv(2 * half, lambda copy: copy.start())
            send_kv(2 * half + 1, lambda copy: copy.start())

        @pl.when(jnp.logical_and(frame == 0, is_first))
        def _():
            scatter(half, lambda copy: copy.start())

    @pl.loop(2 * groups - 2, 2 * groups)
    def _(s):
        forward(s)
        gathered(s)

        @pl.when(s == 2 * groups - 2)
        def _():
            pass_kv(1)

        c = lax.rem(s, chunks)
        qkv(frame_of(1), c * STEP, STEP)

        @pl.when(is_first)
        def _():
            kv_copy(c).start()

    @pl.when(t > 0)
    def _():
        @pl.loop(0, PIECES)
        def _(j):
            @pl.when(j != pos)
            def _():
                await_piece(j).wait_recv()

    factor = math.log2(math.e) / DH**0.5

    def attend(frame, prev_slot):
        @pl.loop(0, heads * halves)
        def _(i):
            head = i // halves
            block_q = lax.rem(i, halves)
            k_at = pl.ds(pl.multiple_of(head * DH, DH), DH)
            v_at = pl.ds(pl.multiple_of(cols + head * DH, DH), DH)
            q = Q[pl.ds(pl.multiple_of(frame * tok + block_q * GROUP, GROUP), GROUP), k_at]
            dims = (((1,), (1,)), ((), ()))
            s0 = lax.dot_general(q, KVB[anchor_slot, :, k_at], dims, preferred_element_type=F32)
            s1 = lax.dot_general(q, KVB[prev_slot, :, k_at], dims, preferred_element_type=F32)
            top = jnp.maximum(jnp.max(s0, axis=-1, keepdims=True), jnp.max(s1, axis=-1, keepdims=True))
            e0 = jnp.exp2((s0 - top) * factor)
            e1 = jnp.exp2((s1 - top) * factor)
            norm = jnp.sum(e0, axis=-1, keepdims=True) + jnp.sum(e1, axis=-1, keepdims=True)
            acc = jnp.dot(e0.astype(BF16), KVB[anchor_slot, :, v_at], preferred_element_type=F32)
            acc += jnp.dot(e1.astype(BF16), KVB[prev_slot, :, v_at], preferred_element_type=F32)
            out[frame, pl.ds(pl.multiple_of(block_q * GROUP, GROUP), GROUP), k_at] = (acc / norm).astype(BF16)

    attend(1, 1)

    @pl.when(t > 0)
    def _():
        for c in range(chunks):
            kv_copy(c).wait_recv()

    attend(0, jnp.where(is_first, 1, 0))

    @pl.loop(0, 2 * chunks)
    def _(s):
        z_copy(s).wait_send()
        c_copy(s).wait_send()
        f_copy(s).wait_send()

    halo_sends(lambda copy: copy.wait_send())

    @pl.when(jnp.logical_or(down_relay, up_relay))
    def _():
        up_out().wait_send()

    @pl.when(t < n_tm - 1)
    def _():
        for c in range(chunks):
            send_kv(c, lambda copy: copy.wait_send())

    @pl.when(kv_relay)
    def _():
        for half in range(halves):
            relay_out(half).wait_send()

    @pl.when(is_first)
    def _():
        for half in range(halves):
            scatter(half, lambda copy: copy.wait_send())

    fan_out(lambda copy: copy.wait_send())


def per_device(frames, taps, w_query, w_key, w_value, q_gain, k_gain):
    count, tok, ch = frames.shape
    depth, cols = w_query.shape
    chunks = tok // STEP
    halves = tok // GROUP
    dma = pltpu.SemaphoreType.DMA
    vmem = pl.BlockSpec(memory_space=pltpu.VMEM)
    anywhere = pl.BlockSpec(memory_space=pl.ANY)
    return pl.pallas_call(
        kernel,
        out_shape=jax.ShapeDtypeStruct((count, tok, cols), BF16),
        in_specs=[anywhere, vmem, vmem, vmem, anywhere, anywhere, anywhere],
        out_specs=vmem,
        scratch_shapes=[
            pltpu.VMEM((4, tok, ch), BF16),
            pltpu.VMEM((4, count * tok, ch), BF16),
            pltpu.VMEM((depth, 3 * cols), BF16),
            pltpu.VMEM((4, tok, 2 * cols), BF16),
            pltpu.VMEM((count * tok, cols), BF16),
            pltpu.VMEM((halves, STEP, 2 * cols), BF16),
            pltpu.VMEM((STEP, ch), BF16),
            dma((3,)),
            dma((chunks,)),
            dma((2, chunks)),
            dma((2, chunks)),
            dma((2 * chunks,)),
            dma((2 * chunks,)),
            dma((2 * chunks,)),
            dma((2 * chunks,)),
            dma((2 * chunks,)),
            dma((2 * chunks,)),
            dma((chunks,)),
            dma((chunks,)),
            dma((halves,)),
            dma((halves,)),
            dma((1,)),
            dma((1,)),
            dma((2, PIECES)),
            dma((PIECES,)),
            dma((PIECES,)),
        ],
        compiler_params=pltpu.CompilerParams(
            collective_id=0, has_side_effects=True, vmem_limit_bytes=62 * 1024 * 1024
        ),
    )(frames, taps, q_gain, k_gain, w_query, w_key, w_value)


def solution(mesh):
    placed = (
        P("tm", None, "head"),
        P(None, "head"),
        P(None, "head"),
        P(None, "head"),
        P(None, "head"),
        P("head"),
        P("head"),
    )
    return jax.shard_map(
        per_device, mesh=mesh, in_specs=placed, out_specs=P("tm", None, "head"), check_vma=False
    )
```
